1024 devices in a mesh: tok: 8 (over z), row: 8 (over x), col: 16 (over y, core).
Axes of the slice: x: 8, y: 8, z: 8, core: 2. Of those that a mesh axis runs over, the one named last changes fastest.
Arguments:
- tokens: bfloat16 [1024, 8192], P('tok', 'row'), may hold values from -6 to 6
- w1_blocks: bfloat16 [8, 16, 8, 128, 128], P('row', 'col'), may hold values from -0.25 to 0.25
- w1_rows: int32 [8, 16, 8], P('row', 'col'), may hold values from 0 to 7
- w1_cols: int32 [8, 16, 8], P('row', 'col'), may hold values from 0 to 15
- w2_blocks: bfloat16 [8, 16, 8, 128, 128], P('row', 'col'), may hold values from -0.125 to 0.125
- w2_hidden: int32 [8, 16, 8], P('row', 'col'), may hold values from 0 to 15
- w2_outs: int32 [8, 16, 8], P('row', 'col'), may hold values from 0 to 7
- grad_out: bfloat16 [1024, 8192], P('tok', 'row'), may hold values from -6 to 6
Outputs:
- output: bfloat16 [1024, 8192], P(('tok', 'col'), 'row')
- grad_in: bfloat16 [1024, 8192], P(('tok', 'col'), 'row')
- grad_w1: float32 [8, 16, 8, 128, 128], P('row', 'col', None, 'tok')
- grad_w2: float32 [8, 16, 8, 128, 128], P('row', 'col', None, 'tok')
The draws below stay inside these ranges and needn't reach their ends.
All inputs are finite; a program needn't handle non-finite values.
Results may differ from the reference program's by a relative error of at most 0.0049.
Values may be sent and summed in bfloat16 or wider, within the bound.
A program may use at most 32 MiB of HBM per device.

```python
import math
import jax
import jax.numpy as jnp
import numpy as np
from jax import lax

D = 8192
FF = 32768
BLK = 128
NB = 8
TOKENS = 1024
RB = 8
CB = 16
FAN1 = 512
FAN2 = 2048
N_ROW = 8
N_COL = 16


def touch_ends(result, own_key, smallest, high):
    dims = result.shape
    index_at = [jax.random.randint(jax.random.fold_in(own_key, axis), (), 0, dims[axis]) for axis in range(len(dims))]
    result = result.at[tuple(index_at)].set(smallest)
    longest = dims.index(max(dims))
    index_at[longest] = (index_at[longest] + 1) % dims[longest]
    return result.at[tuple(index_at)].set(high)


def block_scale(stream_key, extent, split, least, high):
    loudness, own = 1.0, jax.random.fold_in(stream_key, 6)
    for axis_at, parts in split:
        heights = jnp.exp(jax.random.uniform(jax.random.fold_in(own, axis_at), (parts,), jnp.float32, least / len(split), high / len(split)))
        loudness = loudness * jnp.repeat(heights, extent[axis_at] // parts).reshape([-1 if axis == axis_at else 1 for axis in range(len(extent))])
    return loudness


def cumulative_ranks(number_of, skew):
    loads = [(1 << 20) // math.isqrt(grade ** skew) + 1 for grade in range(1, number_of + 1)]
    deviation = 1 + sum(loads) // (1 << 30)
    return np.cumsum(np.array([max(1, weight // deviation) for weight in loads]))


def ranked(rng, shape, number_of, slope):
    grid = cumulative_ranks(number_of, slope)
    pick = jax.random.randint(jax.random.fold_in(rng, 1), shape, 0, int(grid[number_of - 1]))
    rank = jnp.searchsorted(jnp.asarray(grid, jnp.int32), pick, side="right")
    return jax.random.permutation(jax.random.fold_in(rng, 2), number_of)[rank].astype(jnp.int32)


def centred(own_key, extent, deviation, limit, split=(), kind=jnp.bfloat16):
    factor_of = block_scale(own_key, extent, split, -0.22, 0.18) if split else 1.0
    entries = jax.random.normal(own_key, extent, jnp.float32) * deviation * factor_of
    return jnp.minimum(jnp.maximum(entries, -limit), limit).astype(kind)


def setup_inputs(seed: int = 0) -> dict:
    key_list = jax.random.split(jax.random.key(seed), 9)
    tokens = centred(key_list[0], (TOKENS, D), 1.0, 6.0, ((0, 8), (1, 8)))
    w1_blocks = centred(key_list[1], (N_ROW, N_COL, NB, BLK, BLK), FAN1 ** -0.5, 0.25, ((0, 8), (1, 16)))
    w1_rows = touch_ends(jax.random.randint(key_list[2], (N_ROW, N_COL, NB), 0, RB), jax.random.fold_in(key_list[2], 1), 0, RB - 1).astype(jnp.int32)
    w1_cols = touch_ends(ranked(key_list[3], (N_ROW, N_COL, NB), CB, 1), jax.random.fold_in(key_list[3], 3), 0, CB - 1).astype(jnp.int32)
    w2_blocks = centred(key_list[4], (N_ROW, N_COL, NB, BLK, BLK), FAN2 ** -0.5, 0.125, ((0, 8), (1, 16)))
    w2_hidden = touch_ends(jax.random.randint(key_list[5], (N_ROW, N_COL, NB), 0, CB), jax.random.fold_in(key_list[5], 1), 0, CB - 1).astype(jnp.int32)
    w2_outs = touch_ends(ranked(key_list[6], (N_ROW, N_COL, NB), RB, 1), jax.random.fold_in(key_list[6], 3), 0, RB - 1).astype(jnp.int32)
    grad_out = centred(key_list[7], (TOKENS, D), 1.0, 6.0, ((0, 8), (1, 8)))
    return {"tokens": tokens, "w1_blocks": w1_blocks, "w1_rows": w1_rows, "w1_cols": w1_cols, "w2_blocks": w2_blocks, "w2_hidden": w2_hidden, "w2_outs": w2_outs, "grad_out": grad_out}


highest = lax.Precision.HIGHEST

def gelu_value(value):
    return value * (0.5 * (1.0 + jax.scipy.special.erf(value / jnp.sqrt(2.0))))

def gelu_slope(value):
    cdf_part = 0.5 * (1.0 + jax.scipy.special.erf(value / jnp.sqrt(2.0)))
    return cdf_part + value * jnp.exp(-0.5 * value * value) / jnp.sqrt(2.0 * jnp.pi)

def select_blocks(source, indices, count):
    onehot = (indices[:, None] == jnp.arange(count, dtype=jnp.int32)[None, :]).astype(jnp.float32)
    shaped = source.astype(jnp.float32).reshape(source.shape[0], count, BLK)
    return jnp.einsum('kr,trb->ktb', onehot, shaped, precision=highest)

def place_blocks(product, indices, count):
    onehot = (indices[:, None] == jnp.arange(count, dtype=jnp.int32)[None, :]).astype(jnp.float32)
    placed = jnp.einsum('kc,ktj->tcj', onehot, product, precision=highest)
    return placed.reshape(product.shape[1], count * BLK)

def sweep(source, weights, index_in, index_out, in_row, count_in, count_out, total_width, flip):
    rows = source.shape[0]
    form = 'ktb,kjb->ktj' if flip else 'ktb,kbj->ktj'

    def step(total, owner):
        row_id = owner // N_COL
        col_id = owner % N_COL
        in_start = (row_id if in_row else col_id) * (count_in * BLK)
        out_start = (col_id if in_row else row_id) * (count_out * BLK)
        piece = lax.dynamic_slice_in_dim(source, in_start, count_in * BLK, 1)
        taken = select_blocks(piece, index_in[owner], count_in)
        product = jnp.einsum(form, taken, weights[owner].astype(jnp.float32), precision=highest)
        placed = place_blocks(product, index_out[owner], count_out)
        current = lax.dynamic_slice_in_dim(total, out_start, count_out * BLK, 1)
        total = lax.dynamic_update_slice_in_dim(total, current + placed, out_start, 1)
        return (total, None)
    owners = jnp.arange(N_ROW * N_COL, dtype=jnp.int32)
    total, _ = lax.scan(step, jnp.zeros((rows, total_width), jnp.float32), owners)
    return total

def block_grads(left, right, weights_shape, index_left, index_right, left_row, count_left, count_right):

    def step(carry, owner):
        row_id = owner // N_COL
        col_id = owner % N_COL
        left_start = (row_id if left_row else col_id) * (count_left * BLK)
        right_start = (col_id if left_row else row_id) * (count_right * BLK)
        left_piece = lax.dynamic_slice_in_dim(left, left_start, count_left * BLK, 1)
        right_piece = lax.dynamic_slice_in_dim(right, right_start, count_right * BLK, 1)
        left_taken = select_blocks(left_piece, index_left[owner], count_left)
        right_taken = select_blocks(right_piece, index_right[owner], count_right)
        return (carry, jnp.einsum('ktb,ktj->kbj', left_taken, right_taken, precision=highest))
    owners = jnp.arange(N_ROW * N_COL, dtype=jnp.int32)
    _, stacked = lax.scan(step, jnp.zeros((), jnp.float32), owners)
    return stacked.reshape(weights_shape)

def reference(tokens, w1_blocks, w1_rows, w1_cols, w2_blocks, w2_hidden, w2_outs, grad_out):
    owners = N_ROW * N_COL
    first = w1_blocks.reshape(owners, NB, BLK, BLK)
    second = w2_blocks.reshape(owners, NB, BLK, BLK)
    first_rows = w1_rows.reshape(owners, NB)
    first_cols = w1_cols.reshape(owners, NB)
    second_hidden = w2_hidden.reshape(owners, NB)
    second_outs = w2_outs.reshape(owners, NB)
    hidden = sweep(tokens, first, first_rows, first_cols, True, RB, CB, FF, False)
    active = gelu_value(hidden).astype(jnp.bfloat16)
    output = sweep(active, second, second_hidden, second_outs, False, CB, RB, D, False).astype(jnp.bfloat16)
    back = sweep(grad_out, second, second_outs, second_hidden, True, RB, CB, FF, True)
    grad_hidden = (back * gelu_slope(hidden)).astype(jnp.bfloat16)
    grad_in = sweep(grad_hidden, first, first_cols, first_rows, False, CB, RB, D, True).astype(jnp.bfloat16)
    grad_w1 = block_grads(tokens, grad_hidden, w1_blocks.shape, first_rows, first_cols, True, RB, CB)
    grad_w2 = block_grads(active, grad_out, w2_blocks.shape, second_hidden, second_outs, False, CB, RB)
    return (output, grad_in, grad_w1, grad_w2)
```

```python
import functools

import jax
import jax.numpy as jnp
from jax import lax
from jax.experimental import pallas as pl
from jax.experimental.pallas import tpu as pltpu
from jax.sharding import PartitionSpec as P

MESH = pl.DeviceIdType.MESH
F32 = jnp.float32
BF16 = jnp.bfloat16
INV_SQRT2 = 0.7071067811865476
INV_SQRT_2PI = 0.3989422804014327
IDX, HID, BACK, ACT, GRAD, OUT, GIN, GW2, GW1 = range(9)


def far_first(size):
    return sorted(range(1, size), key=lambda d: -min(d, size - d))


def kernel(
    size,
    rows1, cols1, hid2, outs2,
    tok_hbm, w1_hbm, w2_hbm, go_hbm,
    out_ref, gin_ref, gw1_ref, gw2_ref,
    tok_ref, w1_ref, w2_ref, go_ref,
    idx_mine, idx_all, idx_s,
    sh, rh, sb, rb, sa, ra, sg, rg,
    act, slope, prod,
    sy1, ry1, sy2, ry2,
    sz1, rz1, sz2, rz2,
    send_sem, recv_sem, in_sem, idx_sem,
):
    n_tok, n_row, n_col = size
    row_blocks, tokens, _ = tok_ref.shape
    slots, blk = w1_ref.shape[0], w1_ref.shape[2]
    col_blocks, share = act.shape[0], act.shape[1]
    t, r, c = lax.axis_index("tok"), lax.axis_index("row"), lax.axis_index("col")

    def columns(src, dst, first):
        return [
            pltpu.make_async_copy(src.at[:, b * blk : (b + 1) * blk], dst.at[b], in_sem.at[first + b])
            for b in range(row_blocks)
        ]

    first_loads = columns(tok_hbm, tok_ref, 0)
    first_loads.append(pltpu.make_async_copy(w1_hbm, w1_ref, in_sem.at[2 * row_blocks]))
    second_loads = columns(go_hbm, go_ref, row_blocks)
    second_loads.append(pltpu.make_async_copy(w2_hbm, w2_ref, in_sem.at[2 * row_blocks + 1]))
    for load in first_loads + second_loads:
        load.start()

    places = (("row", r, n_row), ("col", c, n_col), ("tok", t, n_tok))
    barrier = pltpu.get_barrier_semaphore()
    for axis, me, count in places:
        for d in far_first(count):
            pl.semaphore_signal(
                barrier, inc=1, device_id={axis: lax.rem(me + d, count)}, device_id_type=MESH
            )

    def send(axis, me, count, src, dst, phase, whole=False):
        for d in far_first(count):
            peer = lax.rem(me + d, count)
            pltpu.make_async_remote_copy(
                src_ref=src if whole else src.at[peer],
                dst_ref=dst.at[me],
                send_sem=send_sem.at[phase],
                recv_sem=recv_sem.at[phase],
                device_id={axis: peer},
                device_id_type=MESH,
            ).start()

    def wait(buf, count, sem):
        span = buf.at[pl.ds(0, count - 1)]
        pltpu.make_async_copy(span, span, sem).wait()

    def dot(a, b, ca, cb):
        return lax.dot_general(a, b, (((ca,), (cb,)), ((), ())), preferred_element_type=F32)

    for k in range(slots):
        idx_mine[pl.ds(k, 1), :] = jnp.full((1, blk), cols1[k], jnp.int32)
        idx_mine[pl.ds(slots + k, 1), :] = jnp.full((1, blk), hid2[k], jnp.int32)
    idx_all[r] = idx_mine[...]

    for load in first_loads:
        load.wait()
    for k in range(slots):
        p = dot(tok_ref[rows1[k]], w1_ref[k], 1, 0)
        sh[:, k] = p.astype(BF16).reshape(n_row, share, blk)
    rh[r] = sh[r]
    for load in second_loads:
        load.wait()
    for k in range(slots):
        p = dot(go_ref[outs2[k]], w2_ref[k], 1, 1)
        sb[:, k] = p.astype(BF16).reshape(n_row, share, blk)
    rb[r] = sb[r]

    pl.semaphore_wait(barrier, n_row + n_col + n_tok - 3)
    send("row", r, n_row, idx_mine, idx_all, IDX, whole=True)
    send("row", r, n_row, sh, rh, HID)
    send("row", r, n_row, sb, rb, BACK)

    wait(idx_all, n_row, recv_sem.at[IDX])
    to_smem = pltpu.make_async_copy(idx_all, idx_s, idx_sem)
    to_smem.start()
    to_smem.wait()

    places_of_block = lax.broadcasted_iota(jnp.int32, (col_blocks, share, blk), 0)

    def place(buf, first):
        def body(s, total):
            q, k = s // slots, s % slots
            where = idx_all[q, pl.ds(first + k, 1), :]
            hit = places_of_block == where[None]
            return total + jnp.where(hit, buf[q, k].astype(F32)[None], 0.0)

        return lax.fori_loop(
            0, n_row * slots, body, jnp.zeros((col_blocks, share, blk), F32)
        )

    def gather(dst, first):
        def body(s, carry):
            q, k = s // slots, s % slots
            dst[q, k] = act[idx_s[q, first + k, 0]]
            return carry

        lax.fori_loop(0, n_row * slots, body, 0)

    wait(rh, n_row, recv_sem.at[HID])
    hidden = place(rh, 0)
    cdf = 0.5 * (1.0 + lax.erf(hidden * INV_SQRT2))
    act[...] = (hidden * cdf).astype(BF16)
    slope[...] = cdf + hidden * jnp.exp(-0.5 * hidden * hidden) * INV_SQRT_2PI
    gather(sa, slots)
    ra[r] = sa[r]
    send("row", r, n_row, sa, ra, ACT)

    wait(rb, n_row, recv_sem.at[BACK])
    act[...] = (place(rb, slots) * slope[...]).astype(BF16)
    gather(sg, 0)
    rg[r] = sg[r]
    send("row", r, n_row, sg, rg, GRAD)

    def scatter_out(index, dst):
        half = row_blocks // 2
        own = tokens // n_col

        def total(b):
            acc = jnp.zeros((tokens, blk), F32)
            for k in range(slots):
                hit = jnp.full((tokens, blk), index[k], jnp.int32) == b
                acc += jnp.where(hit, prod[k], 0.0)
            return acc.reshape(n_col, own, blk)

        for b in range(half):
            both = jnp.concatenate([total(b), total(b + half)], axis=1)
            dst[:, :, b * blk : (b + 1) * blk] = both.astype(BF16)

    wait(ra, n_row, recv_sem.at[ACT])
    for k in range(slots):
        prod[k] = dot(ra[:, k].reshape(tokens, blk), w2_ref[k], 1, 0)
    scatter_out(outs2, sy1)
    ry1[c] = sy1[c]
    send("col", c, n_col, sy1, ry1, OUT)
    for k in range(slots):
        p = dot(ra[:, k].reshape(tokens, blk), go_ref[outs2[k]], 0, 0)
        sz2[:, k] = p.astype(BF16).reshape(n_tok, blk // n_tok, blk)
    rz2[t] = sz2[t]
    send("tok", t, n_tok, sz2, rz2, GW2)

    wait(rg, n_row, recv_sem.at[GRAD])
    for k in range(slots):
        prod[k] = dot(rg[:, k].reshape(tokens, blk), w1_ref[k], 1, 1)
    scatter_out(rows1, sy2)
    ry2[c] = sy2[c]
    send("col", c, n_col, sy2, ry2, GIN)
    for k in range(slots):
        p = dot(tok_ref[rows1[k]], rg[:, k].reshape(tokens, blk), 0, 0)
        sz1[:, k] = p.astype(BF16).reshape(n_tok, blk // n_tok, blk)
    rz1[t] = sz1[t]
    send("tok", t, n_tok, sz1, rz1, GW1)

    def finish_rows(buf, out):
        own = out.shape[0]
        half = out.shape[1] // 2
        total = jnp.sum(buf[...].astype(F32), axis=0).astype(BF16)
        out[:, :half] = total[:own]
        out[:, half:] = total[own:]

    wait(ry1, n_col, recv_sem.at[OUT])
    finish_rows(ry1, out_ref)
    wait(rz2, n_tok, recv_sem.at[GW2])
    gw2_ref[...] = jnp.sum(rz2[...].astype(F32), axis=0)
    wait(ry2, n_col, recv_sem.at[GIN])
    finish_rows(ry2, gin_ref)
    wait(rz1, n_tok, recv_sem.at[GW1])
    gw1_ref[...] = jnp.sum(rz1[...].astype(F32), axis=0)

    wait(idx_all, n_row, send_sem.at[IDX])
    for buf, count, phase in (
        (sh, n_row, HID), (sb, n_row, BACK), (sa, n_row, ACT), (sg, n_row, GRAD),
        (sy1, n_col, OUT), (sy2, n_col, GIN), (sz2, n_tok, GW2), (sz1, n_tok, GW1),
    ):
        wait(buf, count, send_sem.at[phase])


def shards(size, hidden_width, tokens, w1_blocks, w1_rows, w1_cols, w2_blocks, w2_hidden, w2_outs, grad_out):
    n_tok, n_row, n_col = size
    slots, blk = w1_blocks.shape[2], w1_blocks.shape[-1]
    rows, width = tokens.shape
    col_blocks = hidden_width // n_col // blk
    share, own, strip = rows // n_row, rows // n_col, blk // n_tok
    any_spec = pl.BlockSpec(memory_space=pl.ANY)
    smem = pl.BlockSpec(memory_space=pltpu.SMEM)
    vmem = pl.BlockSpec(memory_space=pltpu.VMEM)
    along_row = pltpu.VMEM((n_row, slots, share, blk), BF16)
    along_col = pltpu.VMEM((n_col, 2 * own, width // 2), BF16)
    along_tok = pltpu.VMEM((n_tok, slots, strip, blk), BF16)
    out, gin, gw1, gw2 = pl.pallas_call(
        functools.partial(kernel, size),
        out_shape=(
            jax.ShapeDtypeStruct((own, width), BF16),
            jax.ShapeDtypeStruct((own, width), BF16),
            jax.ShapeDtypeStruct((slots, strip, blk), F32),
            jax.ShapeDtypeStruct((slots, strip, blk), F32),
        ),
        in_specs=[smem] * 4 + [any_spec] * 4,
        out_specs=[vmem] * 4,
        scratch_shapes=[
            pltpu.VMEM((width // blk, rows, blk), BF16),
            pltpu.VMEM((slots, blk, blk), BF16),
            pltpu.VMEM((slots, blk, blk), BF16),
            pltpu.VMEM((width // blk, rows, blk), BF16),
            pltpu.VMEM((2 * slots, blk), jnp.int32),
            pltpu.VMEM((n_row, 2 * slots, blk), jnp.int32),
            pltpu.SMEM((n_row, 2 * slots, blk), jnp.int32),
        ]
        + [along_row] * 8
        + [
            pltpu.VMEM((col_blocks, share, blk), BF16),
            pltpu.VMEM((col_blocks, share, blk), F32),
            pltpu.VMEM((slots, rows, blk), F32),
        ]
        + [along_col] * 4
        + [along_tok] * 4
        + [
            pltpu.SemaphoreType.DMA((9,)),
            pltpu.SemaphoreType.DMA((9,)),
            pltpu.SemaphoreType.DMA((2 * (width // blk) + 2,)),
            pltpu.SemaphoreType.DMA,
        ],
        compiler_params=pltpu.CompilerParams(collective_id=0, has_side_effects=True),
        name="block_sparse_ffn",
    )(
        w1_rows.reshape(slots), w1_cols.reshape(slots), w2_hidden.reshape(slots), w2_outs.reshape(slots),
        tokens, w1_blocks.reshape(slots, blk, blk), w2_blocks.reshape(slots, blk, blk), grad_out,
    )
    return out, gin, gw1.reshape(1, 1, slots, strip, blk), gw2.reshape(1, 1, slots, strip, blk)


def solution(mesh, hidden_width=32768):
    placed = (
        P("tok", "row"),
        P("row", "col", None, None, None),
        P("row", "col", None),
        P("row", "col", None),
        P("row", "col", None, None, None),
        P("row", "col", None),
        P("row", "col", None),
        P("tok", "row"),
    )
    size = tuple(mesh.shape[axis] for axis in ("tok", "row", "col"))
    return jax.shard_map(
        functools.partial(shards, size, hidden_width),
        mesh=mesh,
        in_specs=placed,
        out_specs=(
            P(("tok", "col"), "row"),
            P(("tok", "col"), "row"),
            P("row", "col", None, "tok", None),
            P("row", "col", None, "tok", None),
        ),
        check_vma=False,
    )
```

```python
import functools

import jax
import jax.numpy as jnp
from jax import lax
from jax.experimental import pallas as pl
from jax.experimental.pallas import tpu as pltpu
from jax.sharding import PartitionSpec as P

MESH = pl.DeviceIdType.MESH
F32 = jnp.float32
BF16 = jnp.bfloat16
INV_SQRT2 = 0.7071067811865476
INV_SQRT_2PI = 0.3989422804014327
IDX, IDXC, HID, BACK, ACT, GRAD, OUT, GIN, GW2, GW1 = 0, 1, 2, 3, 4, 6, 8, 10, 12, 14
PHASES = 16


def far_first(size):
    return sorted(range(1, size), key=lambda d: -min(d, size - d))


def kernel(
    size,
    rows1_hbm, cols1_hbm, hid2_hbm, outs2_hbm,
    tok_hbm, w1_hbm, w2_hbm, go_hbm,
    out_hbm, gin_hbm, gw1_hbm, gw2_hbm,
    rows1, cols1, hid2, outs2,
    tok_ref, w1_ref, w2_ref, go_ref,
    out_ref, gin_ref, gw1_ref, gw2_ref,
    key_mine, keys, key_col_mine, keys_col,
    put1, put2, take1, take2, put_rows,
    sh, rh, sb, rb, sa, ra, sg, rg, slope,
    sy1, ry1, sy2, ry2,
    sz1, rz1, sz2, rz2,
    send_sem, recv_sem, in_sem, idx_sem, out_sem,
):
    n_tok, n_row, n_col = size
    row_blocks, tokens, _ = tok_ref.shape
    slots, blk = w1_ref.shape[0], w1_ref.shape[2]
    share = tokens // n_row
    own = tokens // n_col
    half = slots // 2
    t, r, c = lax.axis_index("tok"), lax.axis_index("row"), lax.axis_index("col")

    places = (("row", r, n_row), ("col", c, n_col), ("tok", t, n_tok))
    barrier = pltpu.get_barrier_semaphore()
    for axis, me, count in places:
        for d in far_first(count):
            pl.semaphore_signal(
                barrier, inc=1, device_id={axis: lax.rem(me + d, count)}, device_id_type=MESH
            )

    index_loads = [
        pltpu.make_async_copy(src, dst, idx_sem.at[i])
        for i, (src, dst) in enumerate(
            ((rows1_hbm, rows1), (cols1_hbm, cols1), (hid2_hbm, hid2), (outs2_hbm, outs2))
        )
    ]

    def columns(src, dst, first):
        return [
            pltpu.make_async_copy(src.at[:, b * blk : (b + 1) * blk], dst.at[b], in_sem.at[first + b])
            for b in range(row_blocks)
        ]

    first_loads = columns(tok_hbm, tok_ref, 0)
    first_loads.append(pltpu.make_async_copy(w1_hbm, w1_ref, in_sem.at[2 * row_blocks]))
    second_loads = columns(go_hbm, go_ref, row_blocks)
    second_loads.append(pltpu.make_async_copy(w2_hbm, w2_ref, in_sem.at[2 * row_blocks + 1]))
    for load in index_loads + first_loads + second_loads:
        load.start()

    def copy(src, dst, phase, axis, peer):
        pltpu.make_async_remote_copy(
            src_ref=src,
            dst_ref=dst,
            send_sem=send_sem.at[phase],
            recv_sem=recv_sem.at[phase],
            device_id={axis: peer},
            device_id_type=MESH,
        ).start()

    def wait(span, sem):
        pltpu.make_async_copy(span, span, sem).wait()

    def send_same(axis, me, count, src, dst, phase):
        for d in far_first(count):
            copy(src, dst.at[me], phase, axis, lax.rem(me + d, count))

    def send(axis, me, count, src, dst, phase, lo, n):
        for d in far_first(count):
            peer = lax.rem(me + d, count)
            copy(src.at[peer, pl.ds(lo, n)], dst.at[me, pl.ds(lo, n)], phase, axis, peer)

    def dot(a, b, ca, cb):
        return lax.dot_general(a, b, (((ca,), (cb,)), ((), ())), preferred_element_type=F32)

    for load in index_loads:
        load.wait()

    def key_row(index, first, count, rows, lanes):
        lane = lax.broadcasted_iota(jnp.int32, (1, lanes), 1)
        inner = lax.rem(lane, count * rows)
        key = inner
        for k in range(count):
            inside = (inner >= k * rows) & (inner < (k + 1) * rows)
            key = key + jnp.where(inside, (index[first + k] - k) * rows, 0)
        return key

    lanes, lanes_col = keys.shape[-1], keys_col.shape[-1]
    key_mine[pl.ds(0, 1), :] = key_row(cols1, 0, slots, share, lanes)
    key_mine[pl.ds(1, 1), :] = key_row(hid2, 0, slots, share, lanes)
    for i, (index, first) in enumerate(((outs2, 0), (outs2, half), (rows1, 0), (rows1, half))):
        key_col_mine[pl.ds(i, 1), :] = key_row(index, first, half, own, lanes_col)
    keys[r] = key_mine[...]
    keys_col[c] = key_col_mine[...]

    for load in first_loads:
        load.wait()
    for k in range(slots):
        p = dot(tok_ref[rows1[k]], w1_ref[k], 1, 0)
        sh[:, k] = p.astype(BF16).reshape(n_row, share, blk)
    rh[r] = sh[r]
    pl.semaphore_wait(barrier, n_row + n_col + n_tok - 3)
    send_same("row", r, n_row, key_mine, keys, IDX)
    send("row", r, n_row, sh, rh, HID, 0, slots)
    for load in second_loads:
        load.wait()
    for k in range(slots):
        p = dot(go_ref[outs2[k]], w2_ref[k], 1, 1)
        sb[:, k] = p.astype(BF16).reshape(n_row, share, blk)
    rb[r] = sb[r]
    send("row", r, n_row, sb, rb, BACK, 0, slots)
    send_same("col", c, n_col, key_col_mine, keys_col, IDXC)

    wait(keys.at[pl.ds(0, n_row - 1)], recv_sem.at[IDX])
    held = put1.shape[1]
    held_at = lax.broadcasted_iota(jnp.int32, (held, lanes), 0)

    def build(q, carry):
        for i, (put, take) in enumerate(((put1, take1), (put2, take2))):
            hit = jnp.where(held_at == keys[q, pl.ds(i, 1), :], 1.0, 0.0)
            put[q] = hit.astype(BF16)
            take[q] = hit.T.astype(BF16)
        return carry

    lax.fori_loop(0, n_row, build, 0)

    def place(put, buf):
        total = dot(put[0], buf[0].reshape(slots * share, blk), 1, 0)
        for q in range(1, n_row):
            total += dot(put[q], buf[q].reshape(slots * share, blk), 1, 0)
        return total

    def pick(take, value, dst):
        for q in range(n_row):
            dst[q] = dot(take[q], value, 1, 0).astype(BF16).reshape(slots, share, blk)

    wait(rh.at[pl.ds(0, n_row - 1)], recv_sem.at[HID])
    hidden = place(put1, rh)
    cdf = 0.5 * (1.0 + lax.erf(hidden * INV_SQRT2))
    pick(take2, (hidden * cdf).astype(BF16), sa)
    ra[r] = sa[r]
    send("row", r, n_row, sa, ra, ACT, 0, half)
    send("row", r, n_row, sa, ra, ACT + 1, half, half)
    slope[...] = cdf + hidden * jnp.exp(-0.5 * hidden * hidden) * INV_SQRT_2PI

    wait(keys_col.at[pl.ds(0, n_col - 1)], recv_sem.at[IDXC])
    group = lanes_col // (half * own)
    rows_at = lax.broadcasted_iota(jnp.int32, (row_blocks * own, lanes_col), 0)
    lane = lax.broadcasted_iota(jnp.int32, (1, lanes_col), 1)
    for i in range(4):
        for g in range(n_col // group):
            key = keys_col[g * group, pl.ds(i, 1), :]
            for j in range(1, group):
                key = jnp.where(lane >= j * half * own, keys_col[g * group + j, pl.ds(i, 1), :], key)
            hit = jnp.where(rows_at == key, 1.0, 0.0)
            put_rows[i, :, g * lanes_col : (g + 1) * lanes_col] = hit.astype(BF16)

    wait(rb.at[pl.ds(0, n_row - 1)], recv_sem.at[BACK])
    pick(take1, (place(put2, rb) * slope[...]).astype(BF16), sg)
    rg[r] = sg[r]
    send("row", r, n_row, sg, rg, GRAD, 0, half)
    send("row", r, n_row, sg, rg, GRAD + 1, half, half)

    def rows_out(got, weights, cb, dst, recv, phase, lo):
        for j in range(lo // 2, (lo + half) // 2):
            pair = [
                dot(got[:, k].reshape(tokens, blk), weights[k], 1, cb).reshape(n_col, own, blk)
                for k in (2 * j, 2 * j + 1)
            ]
            dst[:, j] = jnp.concatenate(pair, axis=1).astype(BF16)
        recv[c, pl.ds(lo // 2, half // 2)] = dst[c, pl.ds(lo // 2, half // 2)]
        send("col", c, n_col, dst, recv, phase, lo // 2, half // 2)

    def strips_out(lefts, rights, dst, recv, phase, lo):
        for k in range(lo, lo + half):
            p = dot(lefts(k), rights(k), 0, 0)
            dst[:, k] = p.astype(BF16).reshape(n_tok, blk // n_tok, blk)
        recv[t, pl.ds(lo, half)] = dst[t, pl.ds(lo, half)]
        send("tok", t, n_tok, dst, recv, phase, lo, half)

    def arrived(buf, count, phase, lo, n):
        wait(buf.at[pl.ds(0, count - 1), pl.ds(lo, n)], recv_sem.at[phase])

    def placed_rows(buf, part, which):
        got = buf[:, part * half // 2 : (part + 1) * half // 2].reshape(n_col * half * own, blk)
        return dot(put_rows[which + part], got, 1, 0)

    def write_rows(total, out, out_to, i):
        for b in range(row_blocks):
            out[:, b * blk : (b + 1) * blk] = total[b * own : (b + 1) * own].astype(BF16)
        write = pltpu.make_async_copy(out, out_to, out_sem.at[i])
        write.start()
        return write

    def act_part(part):
        lo = part * half
        arrived(ra, n_row, ACT + part, lo, half)
        rows_out(ra, w2_ref, 0, sy1, ry1, OUT + part, lo)
        strips_out(
            lambda k: ra[:, k].reshape(tokens, blk), lambda k: go_ref[outs2[k]], sz2, rz2, GW2 + part, lo
        )

    def grad_part(part):
        lo = part * half
        arrived(rg, n_row, GRAD + part, lo, half)
        rows_out(rg, w1_ref, 1, sy2, ry2, GIN + part, lo)
        strips_out(
            lambda k: tok_ref[rows1[k]], lambda k: rg[:, k].reshape(tokens, blk), sz1, rz1, GW1 + part, lo
        )

    act_part(0)
    act_part(1)
    grad_part(0)
    for part in range(2):
        arrived(ry1, n_col, OUT + part, part * half // 2, half // 2)
    writes = [write_rows(placed_rows(ry1, 0, 0) + placed_rows(ry1, 1, 0), out_ref, out_hbm, 0)]
    grad_part(1)

    def strips_in(buf, part, phase, out):
        lo = part * half
        arrived(buf, n_tok, phase + part, lo, half)
        out[pl.ds(lo, half)] = jnp.sum(buf[:, lo : lo + half].astype(F32), axis=0)

    def write_strips(out, out_to, i):
        writes.append(pltpu.make_async_copy(out, out_to, out_sem.at[i]))
        writes[-1].start()

    strips_in(rz2, 0, GW2, gw2_ref)
    strips_in(rz2, 1, GW2, gw2_ref)
    write_strips(gw2_ref, gw2_hbm, 3)
    strips_in(rz1, 0, GW1, gw1_ref)
    arrived(ry2, n_col, GIN, 0, half // 2)
    first_rows = placed_rows(ry2, 0, 2)
    strips_in(rz1, 1, GW1, gw1_ref)
    write_strips(gw1_ref, gw1_hbm, 2)
    arrived(ry2, n_col, GIN + 1, half // 2, half // 2)
    writes.append(write_rows(first_rows + placed_rows(ry2, 1, 2), gin_ref, gin_hbm, 1))

    wait(keys.at[pl.ds(0, n_row - 1)], send_sem.at[IDX])
    wait(keys_col.at[pl.ds(0, n_col - 1)], send_sem.at[IDXC])
    wait(sh.at[pl.ds(0, n_row - 1)], send_sem.at[HID])
    wait(sb.at[pl.ds(0, n_row - 1)], send_sem.at[BACK])
    for part in range(2):
        lo = part * half
        for buf, count, phase, at, n in (
            (sa, n_row, ACT, lo, half), (sg, n_row, GRAD, lo, half),
            (sy1, n_col, OUT, lo // 2, half // 2), (sy2, n_col, GIN, lo // 2, half // 2),
            (sz2, n_tok, GW2, lo, half), (sz1, n_tok, GW1, lo, half),
        ):
            wait(buf.at[pl.ds(0, count - 1), pl.ds(at, n)], send_sem.at[phase + part])
    for write in writes:
        write.wait()


def write_results(*refs):
    for src, dst in zip(refs[:4], refs[4:]):
        dst[...] = src[...]


def shards(size, hidden_width, tokens, w1_blocks, w1_rows, w1_cols, w2_blocks, w2_hidden, w2_outs, grad_out):
    n_tok, n_row, n_col = size
    slots, blk = w1_blocks.shape[2], w1_blocks.shape[-1]
    rows, width = tokens.shape
    col_blocks = hidden_width // n_col // blk
    share, own, strip = rows // n_row, rows // n_col, blk // n_tok
    any_spec = pl.BlockSpec(memory_space=pl.ANY)
    vmem = pl.BlockSpec(memory_space=pltpu.VMEM)
    held = col_blocks * share
    lanes, lanes_col = slots * share, max(blk, slots // 2 * own)
    along_row = pltpu.VMEM((n_row, slots, share, blk), BF16)
    along_col = pltpu.VMEM((n_col, slots // 2, 2 * own, blk), BF16)
    along_tok = pltpu.VMEM((n_tok, slots, strip, blk), BF16)
    shapes = (
        jax.ShapeDtypeStruct((own, width), BF16),
        jax.ShapeDtypeStruct((own, width), BF16),
        jax.ShapeDtypeStruct((slots, strip, blk), F32),
        jax.ShapeDtypeStruct((slots, strip, blk), F32),
    )
    results = pl.pallas_call(
        functools.partial(kernel, size),
        out_shape=shapes,
        in_specs=[any_spec] * 8,
        out_specs=[any_spec] * 4,
        scratch_shapes=[pltpu.SMEM((slots,), jnp.int32)] * 4
        + [
            pltpu.VMEM((width // blk, rows, blk), BF16),
            pltpu.VMEM((slots, blk, blk), BF16),
            pltpu.VMEM((slots, blk, blk), BF16),
            pltpu.VMEM((width // blk, rows, blk), BF16),
        ]
        + [pltpu.VMEM(shape.shape, shape.dtype) for shape in shapes]
        + [
            pltpu.VMEM((2, lanes), jnp.int32),
            pltpu.VMEM((n_row, 2, lanes), jnp.int32),
            pltpu.VMEM((4, lanes_col), jnp.int32),
            pltpu.VMEM((n_col, 4, lanes_col), jnp.int32),
            pltpu.VMEM((n_row, held, lanes), BF16),
            pltpu.VMEM((n_row, held, lanes), BF16),
            pltpu.VMEM((n_row, lanes, held), BF16),
            pltpu.VMEM((n_row, lanes, held), BF16),
            pltpu.VMEM((4, width // blk * own, n_col * slots // 2 * own), BF16),
        ]
        + [along_row] * 8
        + [pltpu.VMEM((held, blk), F32)]
        + [along_col] * 4
        + [along_tok] * 4
        + [
            pltpu.SemaphoreType.DMA((PHASES,)),
            pltpu.SemaphoreType.DMA((PHASES,)),
            pltpu.SemaphoreType.DMA((2 * (width // blk) + 2,)),
            pltpu.SemaphoreType.DMA((4,)),
            pltpu.SemaphoreType.DMA((4,)),
        ],
        compiler_params=pltpu.CompilerParams(collective_id=0, has_side_effects=True),
        name="block_sparse_ffn",
    )(
        w1_rows.reshape(slots), w1_cols.reshape(slots), w2_hidden.reshape(slots), w2_outs.reshape(slots),
        tokens, w1_blocks.reshape(slots, blk, blk), w2_blocks.reshape(slots, blk, blk), grad_out,
    )
    out, gin, gw1, gw2 = pl.pallas_call(
        write_results, out_shape=shapes, in_specs=[vmem] * 4, out_specs=[vmem] * 4, name="write_results"
    )(*results)
    return out, gin, gw1.reshape(1, 1, slots, strip, blk), gw2.reshape(1, 1, slots, strip, blk)


def solution(mesh, hidden_width=32768):
    placed = (
        P("tok", "row"),
        P("row", "col", None, None, None),
        P("row", "col", None),
        P("row", "col", None),
        P("row", "col", None, None, None),
        P("row", "col", None),
        P("row", "col", None),
        P("tok", "row"),
    )
    size = tuple(mesh.shape[axis] for axis in ("tok", "row", "col"))
    return jax.shard_map(
        functools.partial(shards, size, hidden_width),
        mesh=mesh,
        in_specs=placed,
        out_specs=(
            P(("tok", "col"), "row"),
            P(("tok", "col"), "row"),
            P("row", "col", None, "tok", None),
            P("row", "col", None, "tok", None),
        ),
        check_vma=False,
    )
```

```python
import functools

import jax
import jax.numpy as jnp
from jax import lax
from jax.experimental import pallas as pl
from jax.experimental.pallas import tpu as pltpu
from jax.sharding import PartitionSpec as P

MESH = pl.DeviceIdType.MESH
F32 = jnp.float32
BF16 = jnp.bfloat16
INV_SQRT2 = 0.7071067811865476
INV_SQRT_2PI = 0.3989422804014327
IDX, IDXC, HID, BACK, ACT, OUT, GW2, GRAD, GIN, GW1 = 0, 1, 2, 3, 4, 8, 12, 16, 20, 24
PHASES = 28


def cut(slots):
    q = slots // 4
    return ((0, 2 * q), (2 * q, 2 * q)), ((0, 2 * q), (2 * q, 2 * q))


def far_first(size):
    return sorted(range(1, size), key=lambda d: -min(d, size - d))


def kernel(
    size,
    rows1_hbm, cols1_hbm, hid2_hbm, outs2_hbm,
    tok_hbm, w1_hbm, w2_hbm, go_hbm,
    out_ref, gin_ref, gw1_ref, gw2_ref,
    rows1, cols1, hid2, outs2,
    tok_ref, w1_ref, w2_ref, go_ref,
    key_mine, keys, key_col_mine, keys_col,
    put1, put2, take1, take2,
    sh, rh, sb, rb, sa, ra, sg, rg, slope,
    sy1, ry1, sy2, ry2,
    sz1, rz1, sz2, rz2,
    send_sem, recv_sem, in_sem, idx_sem, *put_rows,
):
    n_tok, n_row, n_col = size
    row_blocks, tokens, _ = tok_ref.shape
    slots, blk = w1_ref.shape[0], w1_ref.shape[2]
    share = tokens // n_row
    own = tokens // n_col
    act_parts, grad_parts = cut(slots)
    t, r, c = lax.axis_index("tok"), lax.axis_index("row"), lax.axis_index("col")

    index_loads = [
        pltpu.make_async_copy(src, dst, idx_sem.at[i])
        for i, (src, dst) in enumerate(
            ((rows1_hbm, rows1), (cols1_hbm, cols1), (hid2_hbm, hid2), (outs2_hbm, outs2))
        )
    ]

    def columns(src, dst, first):
        return [
            pltpu.make_async_copy(src.at[:, b * blk : (b + 1) * blk], dst.at[b], in_sem.at[first + b])
            for b in range(row_blocks)
        ]

    first_loads = columns(tok_hbm, tok_ref, 0)
    first_loads.append(pltpu.make_async_copy(w1_hbm, w1_ref, in_sem.at[2 * row_blocks]))
    second_loads = columns(go_hbm, go_ref, row_blocks)
    second_loads.append(pltpu.make_async_copy(w2_hbm, w2_ref, in_sem.at[2 * row_blocks + 1]))
    for load in index_loads + first_loads + second_loads:
        load.start()

    places = (("row", r, n_row), ("col", c, n_col), ("tok", t, n_tok))
    barrier = pltpu.get_barrier_semaphore()
    for axis, me, count in places:
        for d in far_first(count):
            pl.semaphore_signal(
                barrier, inc=1, device_id={axis: lax.rem(me + d, count)}, device_id_type=MESH
            )

    def copy(src, dst, phase, axis, peer):
        pltpu.make_async_remote_copy(
            src_ref=src,
            dst_ref=dst,
            send_sem=send_sem.at[phase],
            recv_sem=recv_sem.at[phase],
            device_id={axis: peer},
            device_id_type=MESH,
        ).start()

    def wait(span, sem):
        pltpu.make_async_copy(span, span, sem).wait()

    def send_same(axis, me, count, src, dst, phase):
        for d in far_first(count):
            copy(src, dst.at[me], phase, axis, lax.rem(me + d, count))

    def send(axis, me, count, src, dst, phase, lo, n):
        for d in far_first(count):
            peer = lax.rem(me + d, count)
            copy(src.at[peer, pl.ds(lo, n)], dst.at[me, pl.ds(lo, n)], phase, axis, peer)

    def dot(a, b, ca, cb):
        return lax.dot_general(a, b, (((ca,), (cb,)), ((), ())), preferred_element_type=F32)

    for load in index_loads:
        load.wait()

    def key_row(index, first, count, rows, lanes):
        lane = lax.broadcasted_iota(jnp.int32, (1, lanes), 1)
        inner = lax.rem(lane, count * rows)
        key = inner
        for k in range(count):
            inside = (inner >= k * rows) & (inner < (k + 1) * rows)
            key = key + jnp.where(inside, (index[first + k] - k) * rows, 0)
        return key

    lanes, lanes_col = keys.shape[-1], keys_col.shape[-1]
    key_mine[pl.ds(0, 1), :] = key_row(cols1, 0, slots, share, lanes)
    key_mine[pl.ds(1, 1), :] = key_row(hid2, 0, slots, share, lanes)
    row_parts = [(outs2, *part) for part in act_parts] + [(rows1, *part) for part in grad_parts]
    for i, (index, lo, n) in enumerate(row_parts):
        key_col_mine[pl.ds(i, 1), :] = key_row(index, lo, n, own, lanes_col)
    keys[r] = key_mine[...]
    keys_col[c] = key_col_mine[...]

    for load in first_loads:
        load.wait()
    for k in range(slots):
        p = dot(tok_ref[rows1[k]], w1_ref[k], 1, 0)
        sh[:, k] = p.astype(BF16).reshape(n_row, share, blk)
    rh[r] = sh[r]
    pl.semaphore_wait(barrier, n_row + n_col + n_tok - 3)
    send_same("row", r, n_row, key_mine, keys, IDX)
    send("row", r, n_row, sh, rh, HID, 0, slots)
    for load in second_loads:
        load.wait()
    for k in range(slots):
        p = dot(go_ref[outs2[k]], w2_ref[k], 1, 1)
        sb[:, k] = p.astype(BF16).reshape(n_row, share, blk)
    rb[r] = sb[r]
    send("row", r, n_row, sb, rb, BACK, 0, slots)
    send_same("col", c, n_col, key_col_mine, keys_col, IDXC)

    wait(keys.at[pl.ds(0, n_row - 1)], recv_sem.at[IDX])
    held = put1.shape[1]
    held_at = lax.broadcasted_iota(jnp.int32, (held, lanes), 0)

    def build(q, carry):
        for i, (put, take) in enumerate(((put1, take1), (put2, take2))):
            hit = jnp.where(held_at == keys[q, pl.ds(i, 1), :], 1.0, 0.0)
            put[q] = hit.astype(BF16)
            take[q] = hit.T.astype(BF16)
        return carry

    lax.fori_loop(0, n_row, build, 0)

    def place(put, buf):
        total = dot(put[0], buf[0].reshape(slots * share, blk), 1, 0)
        for q in range(1, n_row):
            total += dot(put[q], buf[q].reshape(slots * share, blk), 1, 0)
        return total

    def pick(take, value, dst, got, phase, parts):
        for i, (lo, n) in enumerate(parts):
            for q in range(n_row):
                rows = take[q, lo * share : (lo + n) * share]
                dst[q, pl.ds(lo, n)] = dot(rows, value, 1, 0).astype(BF16).reshape(n, share, blk)
            send("row", r, n_row, dst, got, phase + i, lo, n)
        got[r] = dst[r]

    wait(rh.at[pl.ds(0, n_row - 1)], recv_sem.at[HID])
    hidden = place(put1, rh)
    cdf = 0.5 * (1.0 + lax.erf(hidden * INV_SQRT2))
    pick(take2, (hidden * cdf).astype(BF16), sa, ra, ACT, act_parts)
    slope[...] = cdf + hidden * jnp.exp(-0.5 * hidden * hidden) * INV_SQRT_2PI

    wait(keys_col.at[pl.ds(0, n_col - 1)], recv_sem.at[IDXC])
    rows_at = lax.broadcasted_iota(jnp.int32, (row_blocks * own, lanes_col), 0)
    lane = lax.broadcasted_iota(jnp.int32, (1, lanes_col), 1)
    for i, (_, _, n) in enumerate(row_parts):
        group = lanes_col // (n * own)
        for g in range(n_col // group):
            key = keys_col[g * group, pl.ds(i, 1), :]
            for j in range(1, group):
                key = jnp.where(lane >= j * n * own, keys_col[g * group + j, pl.ds(i, 1), :], key)
            hit = jnp.where(rows_at == key, 1.0, 0.0)
            put_rows[i][:, g * lanes_col : (g + 1) * lanes_col] = hit.astype(BF16)

    wait(rb.at[pl.ds(0, n_row - 1)], recv_sem.at[BACK])
    pick(take1, (place(put2, rb) * slope[...]).astype(BF16), sg, rg, GRAD, grad_parts)

    def rows_out(got, weights, cb, dst, recv, phase, lo, n):
        for j in range(lo // 2, (lo + n) // 2):
            pair = [
                dot(got[:, k].reshape(tokens, blk), weights[k], 1, cb).reshape(n_col, own, blk)
                for k in (2 * j, 2 * j + 1)
            ]
            dst[:, j] = jnp.concatenate(pair, axis=1).astype(BF16)
        recv[c, pl.ds(lo // 2, n // 2)] = dst[c, pl.ds(lo // 2, n // 2)]
        send("col", c, n_col, dst, recv, phase, lo // 2, n // 2)

    def strips_out(lefts, rights, dst, recv, phase, lo, n):
        for k in range(lo, lo + n):
            p = dot(lefts(k), rights(k), 0, 0)
            dst[:, k] = p.astype(BF16).reshape(n_tok, blk // n_tok, blk)
        recv[t, pl.ds(lo, n)] = dst[t, pl.ds(lo, n)]
        send("tok", t, n_tok, dst, recv, phase, lo, n)

    def arrived(buf, count, phase, lo, n):
        wait(buf.at[pl.ds(0, count - 1), pl.ds(lo, n)], recv_sem.at[phase])

    def rows_in(buf, phase, i, lo, n, put):
        arrived(buf, n_col, phase + i, lo // 2, n // 2)
        got = buf[:, lo // 2 : (lo + n) // 2].reshape(n_col * n * own, blk)
        return dot(put[...], got, 1, 0)

    def write_rows(total, out):
        for b in range(row_blocks):
            out[:, b * blk : (b + 1) * blk] = total[b * own : (b + 1) * own].astype(BF16)

    def strips_in(buf, phase, i, lo, n, out):
        arrived(buf, n_tok, phase + i, lo, n)
        out[pl.ds(lo, n)] = jnp.sum(buf[:, lo : lo + n].astype(F32), axis=0)

    def block(ref):
        return lambda k: ref[:, k].reshape(tokens, blk)

    def act_part(i):
        lo, n = act_parts[i]
        arrived(ra, n_row, ACT + i, lo, n)
        rows_out(ra, w2_ref, 0, sy1, ry1, OUT + i, lo, n)
        strips_out(block(ra), lambda k: go_ref[outs2[k]], sz2, rz2, GW2 + i, lo, n)

    def grad_part(i):
        lo, n = grad_parts[i]
        arrived(rg, n_row, GRAD + i, lo, n)
        rows_out(rg, w1_ref, 1, sy2, ry2, GIN + i, lo, n)
        strips_out(lambda k: tok_ref[rows1[k]], block(rg), sz1, rz1, GW1 + i, lo, n)

    puts_out, puts_gin = put_rows[: len(act_parts)], put_rows[len(act_parts) :]
    for i in range(len(act_parts)):
        act_part(i)
    if len(grad_parts) > 1:
        grad_part(0)
    rows = [rows_in(ry1, OUT, i, *part, puts_out[i]) for i, part in enumerate(act_parts)]
    write_rows(functools.reduce(jnp.add, rows), out_ref)
    for i in range(1 if len(grad_parts) > 1 else 0, len(grad_parts)):
        grad_part(i)
    rows = rows_in(ry2, GIN, 0, *grad_parts[0], puts_gin[0])
    for i, part in enumerate(act_parts):
        strips_in(rz2, GW2, i, *part, gw2_ref)
    strips_in(rz1, GW1, 0, *grad_parts[0], gw1_ref)
    for i in range(1, len(grad_parts)):
        rows += rows_in(ry2, GIN, i, *grad_parts[i], puts_gin[i])
        strips_in(rz1, GW1, i, *grad_parts[i], gw1_ref)
    write_rows(rows, gin_ref)

    wait(keys.at[pl.ds(0, n_row - 1)], send_sem.at[IDX])
    wait(keys_col.at[pl.ds(0, n_col - 1)], send_sem.at[IDXC])
    wait(sh.at[pl.ds(0, n_row - 1)], send_sem.at[HID])
    wait(sb.at[pl.ds(0, n_row - 1)], send_sem.at[BACK])
    for parts, along in (
        (act_parts, ((sa, n_row, ACT, 1), (sy1, n_col, OUT, 2), (sz2, n_tok, GW2, 1))),
        (grad_parts, ((sg, n_row, GRAD, 1), (sy2, n_col, GIN, 2), (sz1, n_tok, GW1, 1))),
    ):
        for buf, count, phase, per in along:
            for i, (lo, n) in enumerate(parts):
                wait(buf.at[pl.ds(0, count - 1), pl.ds(lo // per, n // per)], send_sem.at[phase + i])


def write_results(*refs):
    sources, targets, sem = refs[:4], refs[4:8], refs[8]
    writes = [pltpu.make_async_copy(s, d, sem.at[i]) for i, (s, d) in enumerate(zip(sources, targets))]
    for write in writes:
        write.start()
    for write in writes:
        write.wait()


def shards(size, hidden_width, tokens, w1_blocks, w1_rows, w1_cols, w2_blocks, w2_hidden, w2_outs, grad_out):
    n_tok, n_row, n_col = size
    slots, blk = w1_blocks.shape[2], w1_blocks.shape[-1]
    rows, width = tokens.shape
    col_blocks = hidden_width // n_col // blk
    share, own, strip = rows // n_row, rows // n_col, blk // n_tok
    any_spec = pl.BlockSpec(memory_space=pl.ANY)
    vmem = pl.BlockSpec(memory_space=pltpu.VMEM)
    held = col_blocks * share
    act_parts, grad_parts = cut(slots)
    parts = act_parts + grad_parts
    lanes, lanes_col = slots * share, max(blk, slots // 2 * own)
    along_row = pltpu.VMEM((n_row, slots, share, blk), BF16)
    along_col = pltpu.VMEM((n_col, slots // 2, 2 * own, blk), BF16)
    along_tok = pltpu.VMEM((n_tok, slots, strip, blk), BF16)
    shapes = (
        jax.ShapeDtypeStruct((own, width), BF16),
        jax.ShapeDtypeStruct((own, width), BF16),
        jax.ShapeDtypeStruct((slots, strip, blk), F32),
        jax.ShapeDtypeStruct((slots, strip, blk), F32),
    )
    results = pl.pallas_call(
        functools.partial(kernel, size),
        out_shape=tuple(pltpu.VMEM(shape.shape, shape.dtype) for shape in shapes),
        in_specs=[any_spec] * 8,
        out_specs=[vmem] * 4,
        scratch_shapes=[pltpu.SMEM((slots,), jnp.int32)] * 4
        + [
            pltpu.VMEM((width // blk, rows, blk), BF16),
            pltpu.VMEM((slots, blk, blk), BF16),
            pltpu.VMEM((slots, blk, blk), BF16),
            pltpu.VMEM((width // blk, rows, blk), BF16),
        ]
        + [
            pltpu.VMEM((2, lanes), jnp.int32),
            pltpu.VMEM((n_row, 2, lanes), jnp.int32),
            pltpu.VMEM((len(parts), lanes_col), jnp.int32),
            pltpu.VMEM((n_col, len(parts), lanes_col), jnp.int32),
            pltpu.VMEM((n_row, held, lanes), BF16),
            pltpu.VMEM((n_row, held, lanes), BF16),
            pltpu.VMEM((n_row, lanes, held), BF16),
            pltpu.VMEM((n_row, lanes, held), BF16),
        ]
        + [along_row] * 8
        + [pltpu.VMEM((held, blk), F32)]
        + [along_col] * 4
        + [along_tok] * 4
        + [
            pltpu.SemaphoreType.DMA((PHASES,)),
            pltpu.SemaphoreType.DMA((PHASES,)),
            pltpu.SemaphoreType.DMA((2 * (width // blk) + 2,)),
            pltpu.SemaphoreType.DMA((4,)),
        ]
        + [pltpu.VMEM((width // blk * own, n_col * n * own), BF16) for _, n in parts],
        compiler_params=pltpu.CompilerParams(collective_id=0, has_side_effects=True),
        name="block_sparse_ffn",
    )(
        w1_rows.reshape(slots), w1_cols.reshape(slots), w2_hidden.reshape(slots), w2_outs.reshape(slots),
        tokens, w1_blocks.reshape(slots, blk, blk), w2_blocks.reshape(slots, blk, blk), grad_out,
    )
    out, gin, gw1, gw2 = pl.pallas_call(
        write_results,
        out_shape=shapes,
        in_specs=[vmem] * 4,
        out_specs=[any_spec] * 4,
        scratch_shapes=[pltpu.SemaphoreType.DMA((4,))],
        name="write_results",
    )(*(pltpu.with_memory_space_constraint(held, pltpu.VMEM) for held in results))
    return out, gin, gw1.reshape(1, 1, slots, strip, blk), gw2.reshape(1, 1, slots, strip, blk)


def solution(mesh, hidden_width=32768):
    placed = (
        P("tok", "row"),
        P("row", "col", None, None, None),
        P("row", "col", None),
        P("row", "col", None),
        P("row", "col", None, None, None),
        P("row", "col", None),
        P("row", "col", None),
        P("tok", "row"),
    )
    size = tuple(mesh.shape[axis] for axis in ("tok", "row", "col"))
    return jax.shard_map(
        functools.partial(shards, size, hidden_width),
        mesh=mesh,
        in_specs=placed,
        out_specs=(
            P(("tok", "col"), "row"),
            P(("tok", "col"), "row"),
            P("row", "col", None, "tok", None),
            P("row", "col", None, "tok", None),
        ),
        check_vma=False,
    )
```

```python
import functools

import jax
import jax.numpy as jnp
from jax import lax
from jax.experimental import pallas as pl
from jax.experimental.pallas import tpu as pltpu
from jax.sharding import PartitionSpec as P

MESH = pl.DeviceIdType.MESH
F32 = jnp.float32
BF16 = jnp.bfloat16
INV_SQRT2 = 0.7071067811865476
INV_SQRT_2PI = 0.3989422804014327
IDX, IDXC, HID, BACK, ACT, OUT, GW2, GRAD, GIN, GW1 = 0, 1, 2, 3, 4, 8, 12, 16, 20, 24
PHASES = 28


def cut(slots):
    q = slots // 4
    return ((0, 2 * q), (2 * q, 2 * q)), ((0, 2 * q), (2 * q, 2 * q))


def far_first(size):
    return sorted(range(1, size), key=lambda d: -min(d, size - d))


def kernel(
    size,
    rows1_hbm, cols1_hbm, hid2_hbm, outs2_hbm,
    tok_hbm, w1_hbm, w2_hbm, go_hbm,
    out_ref, gin_ref, gw1_ref, gw2_ref,
    rows1, cols1, hid2, outs2,
    tok_ref, w1_ref, w2_ref, go_ref,
    key_mine, keys, key_col_mine, keys_col,
    put1, put2, take1, take2,
    sh, rh, sb, rb, sa, ra, sg, rg, slope,
    sy1, ry1, sy2, ry2,
    sz1, rz1, sz2, rz2,
    send_sem, recv_sem, in_sem, idx_sem, *put_rows,
):
    n_tok, n_row, n_col = size
    row_blocks, tokens, _ = tok_ref.shape
    slots, blk = w1_ref.shape[0], w1_ref.shape[2]
    share = tokens // n_row
    own = tokens // n_col
    act_parts, grad_parts = cut(slots)
    t, r, c = lax.axis_index("tok"), lax.axis_index("row"), lax.axis_index("col")

    index_loads = [
        pltpu.make_async_copy(src, dst, idx_sem.at[i])
        for i, (src, dst) in enumerate(
            ((rows1_hbm, rows1), (cols1_hbm, cols1), (hid2_hbm, hid2), (outs2_hbm, outs2))
        )
    ]

    def columns(src, dst, first):
        return [
            pltpu.make_async_copy(src.at[:, b * blk : (b + 1) * blk], dst.at[b], in_sem.at[first + b])
            for b in range(row_blocks)
        ]

    first_loads = columns(tok_hbm, tok_ref, 0)
    first_loads.append(pltpu.make_async_copy(w1_hbm, w1_ref, in_sem.at[2 * row_blocks]))
    second_loads = columns(go_hbm, go_ref, row_blocks)
    second_loads.append(pltpu.make_async_copy(w2_hbm, w2_ref, in_sem.at[2 * row_blocks + 1]))
    for load in index_loads + first_loads + second_loads:
        load.start()

    places = (("row", r, n_row), ("col", c, n_col), ("tok", t, n_tok))
    barrier = pltpu.get_barrier_semaphore()
    for axis, me, count in places:
        for d in far_first(count):
            pl.semaphore_signal(
                barrier, inc=1, device_id={axis: lax.rem(me + d, count)}, device_id_type=MESH
            )

    def copy(src, dst, phase, axis, peer):
        pltpu.make_async_remote_copy(
            src_ref=src,
            dst_ref=dst,
            send_sem=send_sem.at[phase],
            recv_sem=recv_sem.at[phase],
            device_id={axis: peer},
            device_id_type=MESH,
        ).start()

    def wait(span, sem):
        pltpu.make_async_copy(span, span, sem).wait()

    def send_same(axis, me, count, src, dst, phase):
        for d in far_first(count):
            copy(src, dst.at[me], phase, axis, lax.rem(me + d, count))

    def send(axis, me, count, src, dst, phase, lo, n):
        for d in far_first(count):
            peer = lax.rem(me + d, count)
            copy(src.at[peer, pl.ds(lo, n)], dst.at[me, pl.ds(lo, n)], phase, axis, peer)

    def dot(a, b, ca, cb):
        return lax.dot_general(a, b, (((ca,), (cb,)), ((), ())), preferred_element_type=F32)

    for load in index_loads:
        load.wait()

    def key_row(index, first, count, rows, lanes):
        lane = lax.broadcasted_iota(jnp.int32, (1, lanes), 1)
        inner = lax.rem(lane, count * rows)
        key = inner
        for k in range(count):
            inside = (inner >= k * rows) & (inner < (k + 1) * rows)
            key = key + jnp.where(inside, (index[first + k] - k) * rows, 0)
        return key

    lanes, lanes_col = keys.shape[-1], keys_col.shape[-1]
    key_mine[pl.ds(0, 1), :] = key_row(cols1, 0, slots, share, lanes)
    key_mine[pl.ds(1, 1), :] = key_row(hid2, 0, slots, share, lanes)
    row_parts = [(outs2, *part) for part in act_parts] + [(rows1, *part) for part in grad_parts]
    for i, (index, lo, n) in enumerate(row_parts):
        key_col_mine[pl.ds(i, 1), :] = key_row(index, lo, n, own, lanes_col)
    keys[r] = key_mine[...]
    keys_col[c] = key_col_mine[...]

    for load in first_loads:
        load.wait()
    for k in range(slots):
        p = dot(tok_ref[rows1[k]], w1_ref[k], 1, 0)
        sh[:, k] = p.astype(BF16).reshape(n_row, share, blk)
    rh[r] = sh[r]
    pl.semaphore_wait(barrier, n_row + n_col + n_tok - 3)
    send_same("row", r, n_row, key_mine, keys, IDX)
    send("row", r, n_row, sh, rh, HID, 0, slots)
    for load in second_loads:
        load.wait()
    for k in range(slots):
        p = dot(go_ref[outs2[k]], w2_ref[k], 1, 1)
        sb[:, k] = p.astype(BF16).reshape(n_row, share, blk)
    rb[r] = sb[r]
    send("row", r, n_row, sb, rb, BACK, 0, slots)
    send_same("col", c, n_col, key_col_mine, keys_col, IDXC)

    wait(keys.at[pl.ds(0, n_row - 1)], recv_sem.at[IDX])
    held = put1.shape[1]
    held_at = lax.broadcasted_iota(jnp.int32, (held, lanes), 0)

    def build(q, carry):
        for i, (put, take) in enumerate(((put1, take1), (put2, take2))):
            hit = jnp.where(held_at == keys[q, pl.ds(i, 1), :], 1.0, 0.0)
            put[q] = hit.astype(BF16)
            take[q] = hit.T.astype(BF16)
        return carry

    lax.fori_loop(0, n_row, build, 0)

    def place(put, buf):
        total = dot(put[0], buf[0].reshape(slots * share, blk), 1, 0)
        for q in range(1, n_row):
            total += dot(put[q], buf[q].reshape(slots * share, blk), 1, 0)
        return total

    def pick(take, value, dst, got, phase, parts):
        for i, (lo, n) in enumerate(parts):
            for q in range(n_row):
                rows = take[q, lo * share : (lo + n) * share]
                dst[q, pl.ds(lo, n)] = dot(rows, value, 1, 0).astype(BF16).reshape(n, share, blk)
            send("row", r, n_row, dst, got, phase + i, lo, n)
        got[r] = dst[r]

    wait(rh.at[pl.ds(0, n_row - 1)], recv_sem.at[HID])
    hidden = place(put1, rh)
    cdf = 0.5 * (1.0 + lax.erf(hidden * INV_SQRT2))
    pick(take2, (hidden * cdf).astype(BF16), sa, ra, ACT, act_parts)
    slope[...] = cdf + hidden * jnp.exp(-0.5 * hidden * hidden) * INV_SQRT_2PI

    wait(keys_col.at[pl.ds(0, n_col - 1)], recv_sem.at[IDXC])
    rows_at = lax.broadcasted_iota(jnp.int32, (row_blocks * own, lanes_col), 0)
    lane = lax.broadcasted_iota(jnp.int32, (1, lanes_col), 1)
    for i, (_, _, n) in enumerate(row_parts):
        group = lanes_col // (n * own)
        for g in range(n_col // group):
            key = keys_col[g * group, pl.ds(i, 1), :]
            for j in range(1, group):
                key = jnp.where(lane >= j * n * own, keys_col[g * group + j, pl.ds(i, 1), :], key)
            hit = jnp.where(rows_at == key, 1.0, 0.0)
            put_rows[i][:, g * lanes_col : (g + 1) * lanes_col] = hit.astype(BF16)

    wait(rb.at[pl.ds(0, n_row - 1)], recv_sem.at[BACK])
    pick(take1, (place(put2, rb) * slope[...]).astype(BF16), sg, rg, GRAD, grad_parts)

    def rows_out(got, weights, cb, dst, recv, phase, lo, n):
        for j in range(lo // 2, (lo + n) // 2):
            pair = [
                dot(got[:, k].reshape(tokens, blk), weights[k], 1, cb).reshape(n_col, own, blk)
                for k in (2 * j, 2 * j + 1)
            ]
            dst[:, j] = jnp.concatenate(pair, axis=1).astype(BF16)
        recv[c, pl.ds(lo // 2, n // 2)] = dst[c, pl.ds(lo // 2, n // 2)]
        send("col", c, n_col, dst, recv, phase, lo // 2, n // 2)

    def strips_out(lefts, rights, dst, recv, phase, lo, n):
        for k in range(lo, lo + n):
            p = dot(lefts(k), rights(k), 0, 0)
            dst[:, k] = p.astype(BF16).reshape(n_tok, blk // n_tok, blk)
        recv[t, pl.ds(lo, n)] = dst[t, pl.ds(lo, n)]
        send("tok", t, n_tok, dst, recv, phase, lo, n)

    def arrived(buf, count, phase, lo, n):
        wait(buf.at[pl.ds(0, count - 1), pl.ds(lo, n)], recv_sem.at[phase])

    def rows_in(buf, phase, i, lo, n, put):
        arrived(buf, n_col, phase + i, lo // 2, n // 2)
        got = buf[:, lo // 2 : (lo + n) // 2].reshape(n_col * n * own, blk)
        return dot(put[...], got, 1, 0)

    def write_rows(total, out):
        for b in range(row_blocks):
            out[:, b * blk : (b + 1) * blk] = total[b * own : (b + 1) * own].astype(BF16)

    def strips_in(buf, phase, i, lo, n, out):
        arrived(buf, n_tok, phase + i, lo, n)
        out[pl.ds(lo, n)] = jnp.sum(buf[:, lo : lo + n].astype(F32), axis=0)

    def block(ref):
        return lambda k: ref[:, k].reshape(tokens, blk)

    def act_part(i):
        lo, n = act_parts[i]
        arrived(ra, n_row, ACT + i, lo, n)
        rows_out(ra, w2_ref, 0, sy1, ry1, OUT + i, lo, n)
        strips_out(block(ra), lambda k: go_ref[outs2[k]], sz2, rz2, GW2 + i, lo, n)

    def grad_part(i):
        lo, n = grad_parts[i]
        arrived(rg, n_row, GRAD + i, lo, n)
        rows_out(rg, w1_ref, 1, sy2, ry2, GIN + i, lo, n)
        strips_out(lambda k: tok_ref[rows1[k]], block(rg), sz1, rz1, GW1 + i, lo, n)

    puts_out, puts_gin = put_rows[: len(act_parts)], put_rows[len(act_parts) :]
    for i in range(len(act_parts)):
        act_part(i)
    if len(grad_parts) > 1:
        grad_part(0)
    for i in range(1 if len(grad_parts) > 1 else 0, len(grad_parts)):
        grad_part(i)
    rows = [rows_in(ry1, OUT, i, *part, puts_out[i]) for i, part in enumerate(act_parts)]
    write_rows(functools.reduce(jnp.add, rows), out_ref)
    rows = rows_in(ry2, GIN, 0, *grad_parts[0], puts_gin[0])
    for i, part in enumerate(act_parts):
        strips_in(rz2, GW2, i, *part, gw2_ref)
    strips_in(rz1, GW1, 0, *grad_parts[0], gw1_ref)
    for i in range(1, len(grad_parts)):
        rows += rows_in(ry2, GIN, i, *grad_parts[i], puts_gin[i])
        strips_in(rz1, GW1, i, *grad_parts[i], gw1_ref)
    write_rows(rows, gin_ref)

    wait(keys.at[pl.ds(0, n_row - 1)], send_sem.at[IDX])
    wait(keys_col.at[pl.ds(0, n_col - 1)], send_sem.at[IDXC])
    wait(sh.at[pl.ds(0, n_row - 1)], send_sem.at[HID])
    wait(sb.at[pl.ds(0, n_row - 1)], send_sem.at[BACK])
    for parts, along in (
        (act_parts, ((sa, n_row, ACT, 1), (sy1, n_col, OUT, 2), (sz2, n_tok, GW2, 1))),
        (grad_parts, ((sg, n_row, GRAD, 1), (sy2, n_col, GIN, 2), (sz1, n_tok, GW1, 1))),
    ):
        for buf, count, phase, per in along:
            for i, (lo, n) in enumerate(parts):
                wait(buf.at[pl.ds(0, count - 1), pl.ds(lo // per, n // per)], send_sem.at[phase + i])


def write_results(*refs):
    sources, targets, sem = refs[:4], refs[4:8], refs[8]
    writes = [pltpu.make_async_copy(s, d, sem.at[i]) for i, (s, d) in enumerate(zip(sources, targets))]
    for write in writes:
        write.start()
    for write in writes:
        write.wait()


def shards(size, hidden_width, tokens, w1_blocks, w1_rows, w1_cols, w2_blocks, w2_hidden, w2_outs, grad_out):
    n_tok, n_row, n_col = size
    slots, blk = w1_blocks.shape[2], w1_blocks.shape[-1]
    rows, width = tokens.shape
    col_blocks = hidden_width // n_col // blk
    share, own, strip = rows // n_row, rows // n_col, blk // n_tok
    any_spec = pl.BlockSpec(memory_space=pl.ANY)
    vmem = pl.BlockSpec(memory_space=pltpu.VMEM)
    held = col_blocks * share
    act_parts, grad_parts = cut(slots)
    parts = act_parts + grad_parts
    lanes, lanes_col = slots * share, max(blk, slots // 2 * own)
    along_row = pltpu.VMEM((n_row, slots, share, blk), BF16)
    along_col = pltpu.VMEM((n_col, slots // 2, 2 * own, blk), BF16)
    along_tok = pltpu.VMEM((n_tok, slots, strip, blk), BF16)
    shapes = (
        jax.ShapeDtypeStruct((own, width), BF16),
        jax.ShapeDtypeStruct((own, width), BF16),
        jax.ShapeDtypeStruct((slots, strip, blk), F32),
        jax.ShapeDtypeStruct((slots, strip, blk), F32),
    )
    results = pl.pallas_call(
        functools.partial(kernel, size),
        out_shape=tuple(pltpu.VMEM(shape.shape, shape.dtype) for shape in shapes),
        in_specs=[any_spec] * 8,
        out_specs=[vmem] * 4,
        scratch_shapes=[pltpu.SMEM((slots,), jnp.int32)] * 4
        + [
            pltpu.VMEM((width // blk, rows, blk), BF16),
            pltpu.VMEM((slots, blk, blk), BF16),
            pltpu.VMEM((slots, blk, blk), BF16),
            pltpu.VMEM((width // blk, rows, blk), BF16),
        ]
        + [
            pltpu.VMEM((2, lanes), jnp.int32),
            pltpu.VMEM((n_row, 2, lanes), jnp.int32),
            pltpu.VMEM((len(parts), lanes_col), jnp.int32),
            pltpu.VMEM((n_col, len(parts), lanes_col), jnp.int32),
            pltpu.VMEM((n_row, held, lanes), BF16),
            pltpu.VMEM((n_row, held, lanes), BF16),
            pltpu.VMEM((n_row, lanes, held), BF16),
            pltpu.VMEM((n_row, lanes, held), BF16),
        ]
        + [along_row] * 8
        + [pltpu.VMEM((held, blk), F32)]
        + [along_col] * 4
        + [along_tok] * 4
        + [
            pltpu.SemaphoreType.DMA((PHASES,)),
            pltpu.SemaphoreType.DMA((PHASES,)),
            pltpu.SemaphoreType.DMA((2 * (width // blk) + 2,)),
            pltpu.SemaphoreType.DMA((4,)),
        ]
        + [pltpu.VMEM((width // blk * own, n_col * n * own), BF16) for _, n in parts],
        compiler_params=pltpu.CompilerParams(collective_id=0, has_side_effects=True),
        name="block_sparse_ffn",
    )(
        w1_rows.reshape(slots), w1_cols.reshape(slots), w2_hidden.reshape(slots), w2_outs.reshape(slots),
        tokens, w1_blocks.reshape(slots, blk, blk), w2_blocks.reshape(slots, blk, blk), grad_out,
    )
    out, gin, gw1, gw2 = pl.pallas_call(
        write_results,
        out_shape=shapes,
        in_specs=[vmem] * 4,
        out_specs=[any_spec] * 4,
        scratch_shapes=[pltpu.SemaphoreType.DMA((4,))],
        name="write_results",
    )(*(pltpu.with_memory_space_constraint(held, pltpu.VMEM) for held in results))
    return out, gin, gw1.reshape(1, 1, slots, strip, blk), gw2.reshape(1, 1, slots, strip, blk)


def solution(mesh, hidden_width=32768):
    placed = (
        P("tok", "row"),
        P("row", "col", None, None, None),
        P("row", "col", None),
        P("row", "col", None),
        P("row", "col", None, None, None),
        P("row", "col", None),
        P("row", "col", None),
        P("tok", "row"),
    )
    size = tuple(mesh.shape[axis] for axis in ("tok", "row", "col"))
    return jax.shard_map(
        functools.partial(shards, size, hidden_width),
        mesh=mesh,
        in_specs=placed,
        out_specs=(
            P(("tok", "col"), "row"),
            P(("tok", "col"), "row"),
            P("row", "col", None, "tok", None),
            P("row", "col", None, "tok", None),
        ),
        check_vma=False,
    )
```

```python
import functools

import jax
import jax.numpy as jnp
from jax import lax
from jax.experimental import pallas as pl
from jax.experimental.pallas import tpu as pltpu
from jax.sharding import PartitionSpec as P

MESH = pl.DeviceIdType.MESH
F32 = jnp.float32
BF16 = jnp.bfloat16
INV_SQRT2 = 0.7071067811865476
INV_SQRT_2PI = 0.3989422804014327
IDX, IDXC, HID, BACK, ACT, OUT, GW2, GRAD, GIN, GW1 = 0, 1, 2, 3, 4, 8, 12, 16, 20, 24
PHASES = 28


def cut(slots):
    q = slots // 4
    return ((0, 2 * q), (2 * q, 2 * q)), ((0, 2 * q), (2 * q, 2 * q))


def far_first(size):
    return sorted(range(1, size), key=lambda d: -min(d, size - d))


def kernel(
    size,
    rows1_hbm, cols1_hbm, hid2_hbm, outs2_hbm,
    tok_hbm, w1_hbm, w2_hbm, go_hbm,
    out_ref, gin_ref, gw1_ref, gw2_ref,
    rows1, cols1, hid2, outs2,
    tok_ref, w1_ref, w2_ref, go_ref,
    key_mine, keys, key_col_mine, keys_col,
    put1, put2, take1, take2,
    sh, rh, sb, rb, sa, ra, sg, rg, slope,
    sy1, ry1, sy2, ry2,
    sz1, rz1, sz2, rz2,
    send_sem, recv_sem, in_sem, idx_sem, *put_rows,
):
    n_tok, n_row, n_col = size
    row_blocks, tokens, _ = tok_ref.shape
    slots, blk = w1_ref.shape[0], w1_ref.shape[2]
    share = tokens // n_row
    own = tokens // n_col
    act_parts, grad_parts = cut(slots)
    t, r, c = lax.axis_index("tok"), lax.axis_index("row"), lax.axis_index("col")

    index_loads = [
        pltpu.make_async_copy(src, dst, idx_sem.at[i])
        for i, (src, dst) in enumerate(
            ((rows1_hbm, rows1), (cols1_hbm, cols1), (hid2_hbm, hid2), (outs2_hbm, outs2))
        )
    ]

    def columns(src, dst, first):
        return [
            pltpu.make_async_copy(src.at[:, b * blk : (b + 1) * blk], dst.at[b], in_sem.at[first + b])
            for b in range(row_blocks)
        ]

    first_loads = columns(tok_hbm, tok_ref, 0)
    first_loads.append(pltpu.make_async_copy(w1_hbm, w1_ref, in_sem.at[2 * row_blocks]))
    second_loads = columns(go_hbm, go_ref, row_blocks)
    second_loads.append(pltpu.make_async_copy(w2_hbm, w2_ref, in_sem.at[2 * row_blocks + 1]))
    for load in index_loads + first_loads + second_loads:
        load.start()

    places = (("row", r, n_row), ("col", c, n_col), ("tok", t, n_tok))
    barrier = pltpu.get_barrier_semaphore()
    for axis, me, count in places:
        for d in far_first(count):
            pl.semaphore_signal(
                barrier, inc=1, device_id={axis: lax.rem(me + d, count)}, device_id_type=MESH
            )

    def copy(src, dst, phase, axis, peer):
        pltpu.make_async_remote_copy(
            src_ref=src,
            dst_ref=dst,
            send_sem=send_sem.at[phase],
            recv_sem=recv_sem.at[phase],
            device_id={axis: peer},
            device_id_type=MESH,
        ).start()

    def wait(span, sem):
        pltpu.make_async_copy(span, span, sem).wait()

    def send_same(axis, me, count, src, dst, phase):
        for d in far_first(count):
            copy(src, dst.at[me], phase, axis, lax.rem(me + d, count))

    def send(axis, me, count, src, dst, phase, lo, n):
        for d in far_first(count):
            peer = lax.rem(me + d, count)
            copy(src.at[peer, pl.ds(lo, n)], dst.at[me, pl.ds(lo, n)], phase, axis, peer)

    def dot(a, b, ca, cb):
        return lax.dot_general(a, b, (((ca,), (cb,)), ((), ())), preferred_element_type=F32)

    for load in index_loads:
        load.wait()

    def key_row(index, first, count, rows, lanes):
        lane = lax.broadcasted_iota(jnp.int32, (1, lanes), 1)
        inner = lax.rem(lane, count * rows)
        key = inner
        for k in range(count):
            inside = (inner >= k * rows) & (inner < (k + 1) * rows)
            key = key + jnp.where(inside, (index[first + k] - k) * rows, 0)
        return key

    lanes, lanes_col = keys.shape[-1], keys_col.shape[-1]
    key_mine[pl.ds(0, 1), :] = key_row(cols1, 0, slots, share, lanes)
    key_mine[pl.ds(1, 1), :] = key_row(hid2, 0, slots, share, lanes)
    row_parts = [(outs2, *part) for part in act_parts] + [(rows1, *part) for part in grad_parts]
    for i, (index, lo, n) in enumerate(row_parts):
        key_col_mine[pl.ds(i, 1), :] = key_row(index, lo, n, own, lanes_col)
    keys[r] = key_mine[...]
    keys_col[c] = key_col_mine[...]

    for load in first_loads:
        load.wait()
    for k in range(slots):
        p = dot(tok_ref[rows1[k]], w1_ref[k], 1, 0)
        sh[:, k] = p.astype(BF16).reshape(n_row, share, blk)
    rh[r] = sh[r]
    pl.semaphore_wait(barrier, n_row + n_col + n_tok - 3)
    send_same("row", r, n_row, key_mine, keys, IDX)
    send("row", r, n_row, sh, rh, HID, 0, slots)
    for load in second_loads:
        load.wait()
    for k in range(slots):
        p = dot(go_ref[outs2[k]], w2_ref[k], 1, 1)
        sb[:, k] = p.astype(BF16).reshape(n_row, share, blk)
    rb[r] = sb[r]
    send("row", r, n_row, sb, rb, BACK, 0, slots)
    send_same("col", c, n_col, key_col_mine, keys_col, IDXC)

    wait(keys.at[pl.ds(0, n_row - 1)], recv_sem.at[IDX])
    held = put1.shape[1]
    held_at = lax.broadcasted_iota(jnp.int32, (held, lanes), 0)

    def build(q, carry):
        for i, (put, take) in enumerate(((put1, take1), (put2, take2))):
            hit = jnp.where(held_at == keys[q, pl.ds(i, 1), :], 1.0, 0.0)
            put[q] = hit.astype(BF16)
            take[q] = hit.T.astype(BF16)
        return carry

    lax.fori_loop(0, n_row, build, 0)

    def place(put, buf):
        total = dot(put[0], buf[0].reshape(slots * share, blk), 1, 0)
        for q in range(1, n_row):
            total += dot(put[q], buf[q].reshape(slots * share, blk), 1, 0)
        return total

    def pick(take, value, dst, got, phase, parts):
        for i, (lo, n) in enumerate(parts):
            for q in range(n_row):
                rows = take[q, lo * share : (lo + n) * share]
                dst[q, pl.ds(lo, n)] = dot(rows, value, 1, 0).astype(BF16).reshape(n, share, blk)
            send("row", r, n_row, dst, got, phase + i, lo, n)
        got[r] = dst[r]

    wait(rh.at[pl.ds(0, n_row - 1)], recv_sem.at[HID])
    hidden = place(put1, rh)
    cdf = 0.5 * (1.0 + lax.erf(hidden * INV_SQRT2))
    pick(take2, (hidden * cdf).astype(BF16), sa, ra, ACT, act_parts)
    slope[...] = cdf + hidden * jnp.exp(-0.5 * hidden * hidden) * INV_SQRT_2PI

    wait(keys_col.at[pl.ds(0, n_col - 1)], recv_sem.at[IDXC])
    rows_at = lax.broadcasted_iota(jnp.int32, (row_blocks * own, lanes_col), 0)
    lane = lax.broadcasted_iota(jnp.int32, (1, lanes_col), 1)
    for i, (_, _, n) in enumerate(row_parts):
        group = lanes_col // (n * own)
        for g in range(n_col // group):
            key = keys_col[g * group, pl.ds(i, 1), :]
            for j in range(1, group):
                key = jnp.where(lane >= j * n * own, keys_col[g * group + j, pl.ds(i, 1), :], key)
            hit = jnp.where(rows_at == key, 1.0, 0.0)
            put_rows[i][:, g * lanes_col : (g + 1) * lanes_col] = hit.astype(BF16)

    wait(rb.at[pl.ds(0, n_row - 1)], recv_sem.at[BACK])
    pick(take1, (place(put2, rb) * slope[...]).astype(BF16), sg, rg, GRAD, grad_parts)

    def rows_out(got, weights, cb, dst, recv, phase, lo, n):
        for j in range(lo // 2, (lo + n) // 2):
            pair = [
                dot(got[:, k].reshape(tokens, blk), weights[k], 1, cb).reshape(n_col, own, blk)
                for k in (2 * j, 2 * j + 1)
            ]
            dst[:, j] = jnp.concatenate(pair, axis=1).astype(BF16)
        recv[c, pl.ds(lo // 2, n // 2)] = dst[c, pl.ds(lo // 2, n // 2)]
        send("col", c, n_col, dst, recv, phase, lo // 2, n // 2)

    def strips_out(lefts, rights, dst, recv, phase, lo, n):
        for k in range(lo, lo + n):
            p = dot(lefts(k), rights(k), 0, 0)
            dst[:, k] = p.astype(BF16).reshape(n_tok, blk // n_tok, blk)
        recv[t, pl.ds(lo, n)] = dst[t, pl.ds(lo, n)]
        send("tok", t, n_tok, dst, recv, phase, lo, n)

    def arrived(buf, count, phase, lo, n):
        wait(buf.at[pl.ds(0, count - 1), pl.ds(lo, n)], recv_sem.at[phase])

    def rows_in(buf, phase, i, lo, n, put):
        arrived(buf, n_col, phase + i, lo // 2, n // 2)
        got = buf[:, lo // 2 : (lo + n) // 2].reshape(n_col * n * own, blk)
        return dot(put[...], got, 1, 0)

    def write_rows(total, out):
        for b in range(row_blocks):
            out[:, b * blk : (b + 1) * blk] = total[b * own : (b + 1) * own].astype(BF16)

    def strips_in(buf, phase, i, lo, n, out):
        arrived(buf, n_tok, phase + i, lo, n)
        out[pl.ds(lo, n)] = jnp.sum(buf[:, lo : lo + n].astype(F32), axis=0)

    def block(ref):
        return lambda k: ref[:, k].reshape(tokens, blk)

    def act_part(i):
        lo, n = act_parts[i]
        arrived(ra, n_row, ACT + i, lo, n)
        rows_out(ra, w2_ref, 0, sy1, ry1, OUT + i, lo, n)
        strips_out(block(ra), lambda k: go_ref[outs2[k]], sz2, rz2, GW2 + i, lo, n)

    def grad_part(i):
        lo, n = grad_parts[i]
        arrived(rg, n_row, GRAD + i, lo, n)
        rows_out(rg, w1_ref, 1, sy2, ry2, GIN + i, lo, n)
        strips_out(lambda k: tok_ref[rows1[k]], block(rg), sz1, rz1, GW1 + i, lo, n)

    puts_out, puts_gin = put_rows[: len(act_parts)], put_rows[len(act_parts) :]
    for i in range(len(act_parts)):
        act_part(i)
    if len(grad_parts) > 1:
        grad_part(0)
    for i in range(1 if len(grad_parts) > 1 else 0, len(grad_parts)):
        grad_part(i)
    rows = [rows_in(ry1, OUT, i, *part, puts_out[i]) for i, part in enumerate(act_parts)]
    write_rows(functools.reduce(jnp.add, rows), out_ref)
    rows = rows_in(ry2, GIN, 0, *grad_parts[0], puts_gin[0])
    for i, part in enumerate(act_parts):
        strips_in(rz2, GW2, i, *part, gw2_ref)
    strips_in(rz1, GW1, 0, *grad_parts[0], gw1_ref)
    for i in range(1, len(grad_parts)):
        rows += rows_in(ry2, GIN, i, *grad_parts[i], puts_gin[i])
        if i == len(grad_parts) - 1:
            write_rows(rows, gin_ref)
        strips_in(rz1, GW1, i, *grad_parts[i], gw1_ref)

    wait(keys.at[pl.ds(0, n_row - 1)], send_sem.at[IDX])
    wait(keys_col.at[pl.ds(0, n_col - 1)], send_sem.at[IDXC])
    wait(sh.at[pl.ds(0, n_row - 1)], send_sem.at[HID])
    wait(sb.at[pl.ds(0, n_row - 1)], send_sem.at[BACK])
    for parts, along in (
        (act_parts, ((sa, n_row, ACT, 1), (sy1, n_col, OUT, 2), (sz2, n_tok, GW2, 1))),
        (grad_parts, ((sg, n_row, GRAD, 1), (sy2, n_col, GIN, 2), (sz1, n_tok, GW1, 1))),
    ):
        for buf, count, phase, per in along:
            for i, (lo, n) in enumerate(parts):
                wait(buf.at[pl.ds(0, count - 1), pl.ds(lo // per, n // per)], send_sem.at[phase + i])


def write_results(*refs):
    sources, targets, sem = refs[:4], refs[4:8], refs[8]
    writes = [pltpu.make_async_copy(s, d, sem.at[i]) for i, (s, d) in enumerate(zip(sources, targets))]
    for write in writes:
        write.start()
    for write in writes:
        write.wait()


def shards(size, hidden_width, tokens, w1_blocks, w1_rows, w1_cols, w2_blocks, w2_hidden, w2_outs, grad_out):
    n_tok, n_row, n_col = size
    slots, blk = w1_blocks.shape[2], w1_blocks.shape[-1]
    rows, width = tokens.shape
    col_blocks = hidden_width // n_col // blk
    share, own, strip = rows // n_row, rows // n_col, blk // n_tok
    any_spec = pl.BlockSpec(memory_space=pl.ANY)
    vmem = pl.BlockSpec(memory_space=pltpu.VMEM)
    held = col_blocks * share
    act_parts, grad_parts = cut(slots)
    parts = act_parts + grad_parts
    lanes, lanes_col = slots * share, max(blk, slots // 2 * own)
    along_row = pltpu.VMEM((n_row, slots, share, blk), BF16)
    along_col = pltpu.VMEM((n_col, slots // 2, 2 * own, blk), BF16)
    along_tok = pltpu.VMEM((n_tok, slots, strip, blk), BF16)
    shapes = (
        jax.ShapeDtypeStruct((own, width), BF16),
        jax.ShapeDtypeStruct((own, width), BF16),
        jax.ShapeDtypeStruct((slots, strip, blk), F32),
        jax.ShapeDtypeStruct((slots, strip, blk), F32),
    )
    results = pl.pallas_call(
        functools.partial(kernel, size),
        out_shape=tuple(pltpu.VMEM(shape.shape, shape.dtype) for shape in shapes),
        in_specs=[any_spec] * 8,
        out_specs=[vmem] * 4,
        scratch_shapes=[pltpu.SMEM((slots,), jnp.int32)] * 4
        + [
            pltpu.VMEM((width // blk, rows, blk), BF16),
            pltpu.VMEM((slots, blk, blk), BF16),
            pltpu.VMEM((slots, blk, blk), BF16),
            pltpu.VMEM((width // blk, rows, blk), BF16),
        ]
        + [
            pltpu.VMEM((2, lanes), jnp.int32),
            pltpu.VMEM((n_row, 2, lanes), jnp.int32),
            pltpu.VMEM((len(parts), lanes_col), jnp.int32),
            pltpu.VMEM((n_col, len(parts), lanes_col), jnp.int32),
            pltpu.VMEM((n_row, held, lanes), BF16),
            pltpu.VMEM((n_row, held, lanes), BF16),
            pltpu.VMEM((n_row, lanes, held), BF16),
            pltpu.VMEM((n_row, lanes, held), BF16),
        ]
        + [along_row] * 8
        + [pltpu.VMEM((held, blk), F32)]
        + [along_col] * 4
        + [along_tok] * 4
        + [
            pltpu.SemaphoreType.DMA((PHASES,)),
            pltpu.SemaphoreType.DMA((PHASES,)),
            pltpu.SemaphoreType.DMA((2 * (width // blk) + 2,)),
            pltpu.SemaphoreType.DMA((4,)),
        ]
        + [pltpu.VMEM((width // blk * own, n_col * n * own), BF16) for _, n in parts],
        compiler_params=pltpu.CompilerParams(collective_id=0, has_side_effects=True),
        name="block_sparse_ffn",
    )(
        w1_rows.reshape(slots), w1_cols.reshape(slots), w2_hidden.reshape(slots), w2_outs.reshape(slots),
        tokens, w1_blocks.reshape(slots, blk, blk), w2_blocks.reshape(slots, blk, blk), grad_out,
    )
    out, gin, gw1, gw2 = pl.pallas_call(
        write_results,
        out_shape=shapes,
        in_specs=[vmem] * 4,
        out_specs=[any_spec] * 4,
        scratch_shapes=[pltpu.SemaphoreType.DMA((4,))],
        name="write_results",
    )(*(pltpu.with_memory_space_constraint(held, pltpu.VMEM) for held in results))
    return out, gin, gw1.reshape(1, 1, slots, strip, blk), gw2.reshape(1, 1, slots, strip, blk)


def solution(mesh, hidden_width=32768):
    placed = (
        P("tok", "row"),
        P("row", "col", None, None, None),
        P("row", "col", None),
        P("row", "col", None),
        P("row", "col", None, None, None),
        P("row", "col", None),
        P("row", "col", None),
        P("tok", "row"),
    )
    size = tuple(mesh.shape[axis] for axis in ("tok", "row", "col"))
    return jax.shard_map(
        functools.partial(shards, size, hidden_width),
        mesh=mesh,
        in_specs=placed,
        out_specs=(
            P(("tok", "col"), "row"),
            P(("tok", "col"), "row"),
            P("row", "col", None, "tok", None),
            P("row", "col", None, "tok", None),
        ),
        check_vma=False,
    )
```
